32 devices in a mesh: expert: 4 (over y, x), context: 8 (over z, core).
Axes of the slice: x: 2, y: 2, z: 4, core: 2. Of those that a mesh axis runs over, the one named last changes fastest.
Arguments:
- tokens: bfloat16 [4, 1024, 768], P('expert', 'context'), may hold values from -6 to 6
- segments: int32 [4, 1024], P('expert', 'context'), may hold values from 0 to 15, never falling along the last dimension, each value on 1 to 512 neighbouring positions
- routes: int32 [4, 1024, 2], P('expert', 'context'), may hold values from 0 to 7, all different within a row
- attn_gain: bfloat16 [768], replicated, may hold values from 0.5 to 1.5
- w_query: bfloat16 [768, 768], replicated, may hold values from -0.21875 to 0.21875
- w_key: bfloat16 [768, 768], replicated, may hold values from -0.21875 to 0.21875
- w_value: bfloat16 [768, 768], replicated, may hold values from -0.21875 to 0.21875
- w_out: bfloat16 [768, 768], replicated, may hold values from -1.25 to 1.25
- ffn_gain: bfloat16 [768], replicated, may hold values from 0.5 to 1.5
- w_router: bfloat16 [768, 8], replicated, may hold values from -0.21875 to 0.21875
- shared_gate: bfloat16 [768, 2048], replicated, may hold values from -0.21875 to 0.21875
- shared_up: bfloat16 [768, 2048], replicated, may hold values from -0.21875 to 0.21875
- shared_down: bfloat16 [2048, 768], replicated, may hold values from -0.125 to 0.125
- expert_gate: bfloat16 [8, 768, 2048], P('expert'), may hold values from -0.21875 to 0.21875
- expert_up: bfloat16 [8, 768, 2048], P('expert'), may hold values from -0.21875 to 0.21875
- expert_down: bfloat16 [8, 2048, 768], P('expert'), may hold values from -0.125 to 0.125
- cotangent: bfloat16 [4, 1024, 768], P('expert', 'context'), may hold values from -6 to 6
Outputs:
- result: bfloat16 [4, 1024, 768], P('expert', 'context')
- d_tokens: float32 [4, 1024, 768], P('expert', 'context')
- grad_attn_gain: float32 [768], replicated
- grad_w_query: float32 [768, 768], replicated
- grad_w_key: float32 [768, 768], replicated
- grad_w_value: float32 [768, 768], replicated
- grad_w_out: float32 [768, 768], replicated
- grad_ffn_gain: float32 [768], replicated
- grad_w_router: float32 [768, 8], replicated
- grad_shared_gate: float32 [768, 2048], replicated
- grad_shared_up: float32 [768, 2048], replicated
- grad_shared_down: float32 [2048, 768], replicated
- grad_expert_gate: float32 [8, 768, 2048], P('expert')
- grad_expert_up: float32 [8, 768, 2048], P('expert')
- grad_expert_down: float32 [8, 2048, 768], P('expert')
The draws below stay inside these ranges and needn't reach their ends.
Inputs may be any that keep to these rules, and one draw needn't show every extreme that they name: `segments`: segment numbers never fall along a sequence; a document spans at most half of 1024 positions. A token's 2 routes name different experts.
All inputs are finite; a program needn't handle non-finite values.
Results may differ from the reference program's by a relative error of at most 0.025.
Values may be sent and summed in bfloat16 or wider, within the bound.
No kernel may reach another device: no remote copies, remote signals or barrier semaphores. Data moves between devices by JAX's collectives and lax.ppermute only.
A program may use at most 320 MiB of HBM per device.

```python
import math
import jax
import jax.numpy as jnp
import numpy as np
from jax import lax

D = 768
HEADS = 12
HEAD = 64
FF = 2048
TOP = 2
STRETCH = 128
SEQ_DEV = 1
EXPERTS = 8
SEQS = 4
LENGTH = 1024
CAP = 36
N_EXPERT = 4
N_CONTEXT = 8


def steps_of(stream_key, extent, pieces, low, top_value):
    level = 1.0
    for position, blocks in pieces:
        steps = jax.random.uniform(jax.random.fold_in(jax.random.fold_in(stream_key, 6), position), (blocks,), jnp.float32, low / len(pieces), top_value / len(pieces))
        level = level * jnp.repeat(jnp.exp(steps), extent[position] // blocks).reshape((-1,) + (1,) * (len(extent) - 1 - position))
    return level


def different_ones(stream_key, rows, count, top, lift):
    sequence = jax.random.permutation(jax.random.fold_in(stream_key, 1), count)
    favour = sequence
    for power in range(3):
        favour = favour * favour // count
    favour = favour * lift // count
    tickets = jax.random.randint(jax.random.fold_in(stream_key, 2), (rows, count), 0, 4096) + favour
    fixed_rows = jax.random.permutation(jax.random.fold_in(stream_key, 3), rows)[jnp.arange(count) % rows]
    tickets = jnp.where(jnp.arange(rows)[:, None] == fixed_rows[None, :], 1 << 14, tickets)
    score = tickets * count + jnp.arange(count)
    return lax.top_k(score.astype(jnp.int32), top)[1].astype(jnp.int32)


def split_up(count, total, bound, slope):
    portions = [(1 << 20) // math.isqrt(grade ** slope) + 1 for grade in range(2, count + 1)]
    spare, given = total - bound - (count - 1), [1] * (count - 1)
    while spare > 0:
        movable = [i for i in range(count - 1) if given[i] < bound]
        mass, left = sum([portions[i] for i in movable]), spare
        for i in movable:
            addition = min(bound - given[i], max(1, left * portions[i] // mass), spare)
            given[i] = given[i] + addition
            spare = spare - addition
    return np.array([bound] + given)


def ragged_sizes(rng, amount, total, reach, lean):
    if amount == 2:
        one = jax.random.randint(rng, (), max(1, total - reach), min(reach, total - 1) + 1)
        return jnp.stack([one, total - one])
    sizes = jnp.asarray(split_up(amount, total, reach, lean), jnp.int32)
    twos = (amount - 1) // 2
    donor, receiver = sizes[1:1 + 2 * twos:2], sizes[2:2 + 2 * twos:2]
    margin = jnp.minimum(donor - 1, reach - receiver)
    moved = jax.random.randint(jax.random.fold_in(rng, 1), (twos,), 0, 1 << 20) % (margin + 1)
    sizes = sizes.at[1:1 + 2 * twos:2].set(donor - moved).at[2:2 + 2 * twos:2].set(receiver + moved)
    return sizes[jax.random.permutation(jax.random.fold_in(rng, 2), amount)]


def normal_values(key, extent, scale, bound, pieces=(), kind=jnp.bfloat16):
    level = steps_of(key, extent, pieces, -0.22, 0.18) if pieces else 1.0
    values = jax.random.normal(key, extent, jnp.float32) * scale * level
    return jnp.minimum(jnp.maximum(values, -bound), bound).astype(kind)


def setup_inputs(seed: int = 0) -> dict:
    key_list = jax.random.split(jax.random.key(seed), 18)
    return {
        "tokens": normal_values(key_list[0], (SEQS, LENGTH, D), 1.0, 6.0, ((0, 4), (1, 8))),
        "segments": jax.vmap(lambda own: jnp.searchsorted(jnp.cumsum(ragged_sizes(own, 16, LENGTH, LENGTH // 2, 2)), jnp.arange(LENGTH), side="right"))(jax.random.split(key_list[1], SEQS)).reshape((SEQS, LENGTH)).astype(jnp.int32),
        "routes": different_ones(key_list[2], SEQS * LENGTH, EXPERTS, TOP, 2048).reshape((SEQS, LENGTH, TOP)),
        "attn_gain": jnp.clip(1.0 + 0.1 * jax.random.normal(key_list[3], (D,), jnp.float32), 0.5, 1.5).astype(jnp.bfloat16),
        "w_query": normal_values(key_list[4], (D, D), D ** -0.5, 0.21875),
        "w_key": normal_values(key_list[5], (D, D), D ** -0.5, 0.21875),
        "w_value": normal_values(key_list[6], (D, D), D ** -0.5, 0.21875),
        "w_out": normal_values(key_list[7], (D, D), (D // 32) ** -0.5, 1.25),
        "ffn_gain": jnp.clip(1.0 + 0.1 * jax.random.normal(key_list[8], (D,), jnp.float32), 0.5, 1.5).astype(jnp.bfloat16),
        "w_router": normal_values(key_list[9], (D, EXPERTS), D ** -0.5, 0.21875),
        "shared_gate": normal_values(key_list[10], (D, FF), D ** -0.5, 0.21875),
        "shared_up": normal_values(key_list[11], (D, FF), D ** -0.5, 0.21875),
        "shared_down": normal_values(key_list[12], (FF, D), FF ** -0.5, 0.125),
        "expert_gate": normal_values(key_list[13], (EXPERTS, D, FF), D ** -0.5, 0.21875, ((0, 4),)),
        "expert_up": normal_values(key_list[14], (EXPERTS, D, FF), D ** -0.5, 0.21875, ((0, 4),)),
        "expert_down": normal_values(key_list[15], (EXPERTS, FF, D), FF ** -0.5, 0.125, ((0, 4),)),
        "cotangent": normal_values(key_list[16], (SEQS, LENGTH, D), 1.0, 6.0, ((0, 4), (1, 8))),
    }


EPSILON = 1e-06
MASKED = -1e+30
HIGHEST = lax.Precision.HIGHEST

@jax.custom_vjp
def low(v):
    return lax.optimization_barrier(v.astype(jnp.bfloat16)).astype(jnp.float32)

@jax.custom_vjp
def low_back(v):
    return v

def low_keep(v):
    return (low(v), None)

def low_pass(kept, grad):
    return (grad,)

def back_keep(v):
    return (v, None)

def back_low(kept, grad):
    return (low(grad),)
low.defvjp(low_keep, low_pass)
low_back.defvjp(back_keep, back_low)

def matmul(left, weight):
    return jnp.einsum('...d,de->...e', left, weight, precision=HIGHEST)

def rmsnorm(values, gain):
    return values * lax.rsqrt(lax.optimization_barrier(jnp.mean(values * values, -1, keepdims=True)) + EPSILON) * gain

def rope_table(positions, head_dim):
    half_dim = head_dim // 2
    frequency = jnp.exp(jnp.arange(half_dim, dtype=jnp.float32) * (-2.0 * math.log(10000.0) / head_dim))
    angles = positions.astype(jnp.float32)[:, None] * frequency[None, :]
    return (jnp.cos(angles), jnp.sin(angles))

def rotate(values, cosines, sine_table, turning):
    half_dim = values.shape[-1] // 2
    former = values[..., :half_dim]
    latter = values[..., half_dim:]
    cos_part = cosines[:, None, :]
    sin_part = turning * sine_table[:, None, :]
    return jnp.concatenate([former * cos_part - latter * sin_part, latter * cos_part + former * sin_part], -1)

def to_groups(values):
    trailing = values.shape[2:]
    values = values.reshape((N_EXPERT, SEQ_DEV, N_CONTEXT, STRETCH) + trailing)
    values = jnp.moveaxis(values, 2, 1)
    return values.reshape((N_EXPERT * N_CONTEXT, SEQ_DEV * STRETCH) + trailing)

def from_groups(values):
    trailing = values.shape[2:]
    values = values.reshape((N_EXPERT, N_CONTEXT, SEQ_DEV, STRETCH) + trailing)
    values = jnp.moveaxis(values, 1, 2)
    return values.reshape((SEQS, LENGTH) + trailing)

def slot_tables(routes):
    group_count = N_EXPERT * N_CONTEXT
    assigned = to_groups(routes).reshape(group_count, SEQ_DEV * STRETCH * TOP)
    onehot = (assigned[:, :, None] == jnp.arange(EXPERTS, dtype=jnp.int32)[None, None, :]).astype(jnp.int32)
    before = jnp.cumsum(onehot, 1) - onehot
    place = lax.optimization_barrier(jnp.sum(before * onehot, -1))
    slot = jnp.where(place < CAP, assigned * CAP + place, EXPERTS * CAP).astype(jnp.int32)

    def invert(slot_row):
        order = jnp.zeros((EXPERTS * CAP + 1,), jnp.int32).at[slot_row].set(jnp.arange(SEQ_DEV * STRETCH * TOP, dtype=jnp.int32))
        filled = jnp.zeros((EXPERTS * CAP + 1,), jnp.int32).at[slot_row].set(1)
        return (order[:EXPERTS * CAP], filled[:EXPERTS * CAP])
    order, filled = jax.vmap(invert)(slot)
    return (slot, order, filled)

def attend_rows(query_rows, keys_all, values_all, seg_rows, seg_all, row_pos):
    score_scale = HEAD ** (-0.5)
    scores = low_back(jnp.einsum('qhd,khd->hqk', query_rows, keys_all, precision=HIGHEST) * score_scale)
    key_pos = jnp.arange(LENGTH, dtype=jnp.int32)
    allowed = (seg_rows[None, :, None] == seg_all[None, None, :]) & (key_pos[None, None, :] <= row_pos[None, :, None])
    weights = low(jax.nn.softmax(jnp.where(allowed, scores, MASKED), -1))
    return jnp.einsum('hqk,khd->qhd', weights, values_all, precision=HIGHEST)

def attend_sequence(packed):
    queries, keys, values, segment_row = packed
    block_rows = math.gcd(LENGTH, 512)
    block_count = LENGTH // block_rows

    def one_block(block_args):
        return attend_rows(block_args[0], keys, values, block_args[1], segment_row, block_args[2])
    positions = jnp.arange(LENGTH, dtype=jnp.int32).reshape(block_count, block_rows)
    outcome = lax.map(jax.checkpoint(one_block), (queries.reshape(block_count, block_rows, HEADS, HEAD), segment_row.reshape(block_count, block_rows), positions))
    return outcome.reshape(LENGTH, HEADS, HEAD)

def rows_per_expert(packed):
    rows_in, gate_weight, up_weight, down_weight = packed
    gate_value = low_back(matmul(rows_in, gate_weight))
    up_value = low_back(matmul(rows_in, up_weight))
    hidden = low(jax.nn.silu(gate_value) * up_value)
    return low(low_back(matmul(hidden, down_weight)))

def pick_rows(table, indices):
    return table[indices]

def take_rows(table, indices):
    return jnp.take(table, indices, axis=0, mode='fill', fill_value=0.0)

def reference(tokens, segments, routes, attn_gain, w_query, w_key, w_value, w_out, ffn_gain, w_router, shared_gate, shared_up, shared_down, expert_gate, expert_up, expert_down, cotangent):
    slot, order, filled = slot_tables(routes)
    group_count = N_EXPERT * N_CONTEXT
    cosines, sine_table = rope_table(jnp.arange(LENGTH, dtype=jnp.int32), HEAD)
    shape4 = (SEQS, LENGTH, HEADS, HEAD)

    def forward_pass(layer_inputs, attention_norm_gain, query_weight_matrix, key_weight_matrix, value_weight_matrix, output_weight_matrix, feed_norm_gain, router_weight_matrix, shared_gate_matrix, shared_up_matrix, shared_down_matrix, expert_gate_matrix, expert_up_matrix, expert_down_matrix):
        normed_a = low(rmsnorm(layer_inputs, attention_norm_gain))
        queries = low(rotate(low_back(matmul(normed_a, query_weight_matrix)).reshape(shape4), cosines, sine_table, 1.0))
        keys = low(rotate(low_back(matmul(normed_a, key_weight_matrix)).reshape(shape4), cosines, sine_table, 1.0))
        values = low(low_back(matmul(normed_a, value_weight_matrix))).reshape(shape4)
        attended = lax.map(jax.checkpoint(attend_sequence), (queries, keys, values, segments)).reshape(SEQS, LENGTH, D)
        attended = low(low_back(attended))
        hidden1 = layer_inputs + low_back(matmul(attended, output_weight_matrix))
        normed_b = low(rmsnorm(hidden1, feed_norm_gain))
        gate_sh = low_back(matmul(normed_b, shared_gate_matrix))
        up_sh = low_back(matmul(normed_b, shared_up_matrix))
        hidden_sh = low(jax.nn.silu(gate_sh) * up_sh)
        shared_out = low_back(matmul(hidden_sh, shared_down_matrix))
        logits = matmul(normed_b, router_weight_matrix)
        gates = jax.nn.softmax(jnp.take_along_axis(logits, routes, -1), -1)
        grouped = to_groups(normed_b)
        expert_input_rows = jax.vmap(pick_rows)(grouped, order // TOP)
        expert_input_rows = low_back(jnp.where(filled[..., None] > 0, expert_input_rows, 0.0))
        expert_input_rows = jnp.moveaxis(expert_input_rows.reshape(group_count, EXPERTS, CAP, D), 1, 0).reshape(EXPERTS, group_count * CAP, D)
        expert_output_rows = lax.map(jax.checkpoint(rows_per_expert), (expert_input_rows, expert_gate_matrix, expert_up_matrix, expert_down_matrix))
        expert_output_rows = jnp.moveaxis(expert_output_rows.reshape(EXPERTS, group_count, CAP, D), 0, 1).reshape(group_count, EXPERTS * CAP, D)
        returned = jax.vmap(take_rows)(expert_output_rows, slot)
        returned = from_groups(returned.reshape(group_count, SEQ_DEV * STRETCH, TOP, D))
        moe = lax.optimization_barrier(jnp.sum(gates[..., None] * returned, 2))
        return hidden1 + shared_out + moe
    floats = (tokens, attn_gain, w_query, w_key, w_value, w_out, ffn_gain, w_router, shared_gate, shared_up, shared_down, expert_gate, expert_up, expert_down)
    floats = tuple((item.astype(jnp.float32) for item in floats))
    output, pullback = jax.vjp(forward_pass, *floats)
    grads = pullback(cotangent.astype(jnp.float32))
    return (output.astype(jnp.bfloat16), grads[0], grads[1], grads[2], grads[3], grads[4], grads[5], grads[6], grads[7], grads[8], grads[9], grads[10], grads[11], grads[12], grads[13])
```

```python
import math

import jax
import jax.numpy as jnp
from jax import lax
from jax.sharding import PartitionSpec as P

HEADS = 12
HEAD = 64
TOP = 2
EPSILON = 1e-06
MASKED = -1e30
LANES = 128
BF = jnp.bfloat16
F32 = jnp.float32


def mm(a, b):
    return jnp.dot(a, b, preferred_element_type=F32)


def mm_t(a, b):
    return lax.dot_general(a, b, (((1,), (1,)), ((), ())), preferred_element_type=F32)


def tmm(a, b):
    return lax.dot_general(a, b, (((0,), (0,)), ((), ())), preferred_element_type=F32)


def rope_table(positions):
    half = HEAD // 2
    frequency = jnp.exp(jnp.arange(half, dtype=F32) * (-2.0 * math.log(10000.0) / HEAD))
    angles = positions.astype(F32)[:, None] * frequency[None, :]
    return jnp.cos(angles), jnp.sin(angles)


def rotate(values, cosines, sines, turning):
    rows = values.shape[0]
    v = values.reshape(rows, HEADS, HEAD)
    former, latter = v[..., : HEAD // 2], v[..., HEAD // 2 :]
    c, s = cosines[:, None, :], turning * sines[:, None, :]
    return jnp.concatenate([former * c - latter * s, latter * c + former * s], -1).reshape(rows, -1)


def heads_of(values):
    return values.reshape(values.shape[0], HEADS, HEAD)


def silu_parts(v):
    s = jax.nn.sigmoid(v)
    return v * s, s * (1.0 + v * (1.0 - s))


def split3(v):
    a = v.astype(BF)
    r = v - a.astype(F32)
    b = r.astype(BF)
    return a, b, (r - b.astype(F32)).astype(BF)


def per_device(
    tokens, segments, routes, attn_gain, w_query, w_key, w_value, w_out, ffn_gain, w_router,
    shared_gate, shared_up, shared_down, expert_gate, expert_up, expert_down, cotangent,
):
    _, stretch, width = tokens.shape
    n_expert = lax.axis_size("expert")
    n_context = lax.axis_size("context")
    chips = n_context // 2
    back = n_context // 4
    me_c = lax.axis_index("context")
    local = expert_gate.shape[0]
    experts = n_expert * local
    cap = (9 * stretch * TOP + 8 * experts - 1) // (8 * experts)
    hidden = shared_gate.shape[1]
    scale = HEAD ** (-0.5)
    pair_groups = [[2 * i, 2 * i + 1] for i in range(chips)]
    chip_groups = [[2 * i + k for i in range(chips)] for k in range(2)]
    swap = [(c, c ^ 1) for c in range(n_context)]

    def up(d):
        return [(c, c + 2 * d) for c in range(n_context - 2 * d)]

    def down(d):
        return [(c + 2 * d, c) for c in range(n_context - 2 * d)]

    def window(block, steps):
        mine = jnp.stack([block] + [lax.ppermute(block, "context", steps(d)) for d in range(1, back + 1)])
        other = lax.ppermute(mine, "context", swap)
        return jnp.concatenate([mine, other], 0)

    def window_blocks(sign):
        d = 2 * sign * jnp.arange(back + 1, dtype=jnp.int32)
        return jnp.concatenate([me_c + d, (me_c ^ 1) + d])

    def positions_of(blocks):
        return (blocks[:, None] * stretch + jnp.arange(stretch, dtype=jnp.int32)[None, :]).reshape(-1)

    tok = tokens[0]
    seg = segments[0]
    dy = cotangent[0]
    dyf = dy.astype(F32)
    seg_rows = jnp.pad(seg[None, :].astype(BF), ((0, 7), (0, width - stretch)))
    packet = jnp.concatenate([tok, seg_rows], 0)
    low_win = window(packet, up)
    high_win = window(packet, down)
    nwin = 2 * (back + 1)

    def unpack(win):
        return win[:, :stretch].reshape(nwin * stretch, width), win[:, stretch, :stretch].astype(jnp.int32).reshape(-1)

    low_tok, low_seg = unpack(low_win)
    high_tok, high_seg = unpack(high_win)
    low_pos = positions_of(window_blocks(-1))
    high_pos = positions_of(window_blocks(1))
    own_pos = me_c * stretch + jnp.arange(stretch, dtype=jnp.int32)
    gain_a = attn_gain.astype(F32)
    gain_b = ffn_gain.astype(F32)

    def norm_in(rows):
        x = rows.astype(F32)
        return (x * lax.rsqrt(jnp.mean(x * x, -1, keepdims=True) + EPSILON) * gain_a).astype(BF)

    low_na = norm_in(low_tok)
    na = low_na[:stretch]
    kw = rotate(mm(low_na, w_key), *rope_table(low_pos), 1.0).astype(BF)
    vw = mm(low_na, w_value).astype(BF)
    q = rotate(mm(na, w_query), *rope_table(own_pos), 1.0).astype(BF)
    scores = jnp.einsum("qhd,khd->hqk", heads_of(q), heads_of(kw), preferred_element_type=F32) * scale
    allowed = (seg[:, None] == low_seg[None, :]) & (low_pos[None, :] <= own_pos[:, None]) & (low_pos[None, :] >= 0)
    scores = jnp.where(allowed[None], scores, MASKED)
    peak = jnp.max(scores, -1, keepdims=True)
    e = jnp.where(allowed[None], jnp.exp(scores - peak), 0.0)
    total = jnp.sum(e, -1, keepdims=True)
    lse = (peak + jnp.log(total))[..., 0].T
    att_f = (jnp.einsum("hqk,khd->qhd", e.astype(BF), heads_of(vw), preferred_element_type=F32) / total[..., 0].T[..., None]).reshape(stretch, width)
    att = att_f.astype(BF)
    tokf = tok.astype(F32)
    h1 = tokf + mm(att, w_out)
    rstd_b = lax.rsqrt(jnp.mean(h1 * h1, -1, keepdims=True) + EPSILON)
    n_b = h1 * rstd_b
    nb = (n_b * gain_b).astype(BF)

    assigned = routes[0].reshape(stretch * TOP)
    onehot = (assigned[:, None] == jnp.arange(experts, dtype=jnp.int32)[None, :])
    row_i = jnp.arange(stretch * TOP, dtype=jnp.int32)
    earlier = (row_i[:, None] > row_i[None, :]).astype(BF)
    before = mm(earlier, onehot.astype(BF))
    place = jnp.sum(jnp.where(onehot, before, 0.0), -1).astype(jnp.int32)
    slot = jnp.where(place < cap, assigned * cap + place, experts * cap).reshape(stretch, TOP)
    slots = experts * cap
    slot_i = jnp.arange(slots, dtype=jnp.int32)
    pick = [(slot_i[:, None] == slot[None, :, r]) for r in range(TOP)]
    pick_b = [p.astype(BF) for p in pick]
    pick_any = (pick[0] | pick[1]).astype(BF)

    logits = mm(nb, w_router)
    route_hot = (routes[0][:, :, None] == jnp.arange(experts, dtype=jnp.int32))
    chosen = jnp.sum(jnp.where(route_hot, logits[:, None, :], 0.0), -1)
    gates = jax.nn.softmax(chosen, -1)

    gate_cols = jnp.stack([jnp.stack(split3(gates[:, r]), -1) for r in range(TOP)])
    gate_cols = jnp.pad(gate_cols, ((0, 0), (0, 0), (0, LANES - 3)))
    out_rows = mm(pick_any, nb).astype(BF)
    out_gates = (mm(pick_b[0], gate_cols[0]) + mm(pick_b[1], gate_cols[1])).astype(BF)
    outgoing = jnp.concatenate([out_rows, out_gates], -1).reshape(n_expert, local * cap, width + LANES)
    x_in = lax.all_to_all(outgoing, "expert", 0, 0, tiled=True)
    dy_out = mm(pick_any, dy).astype(BF).reshape(n_expert, local * cap, width)
    dy_in = lax.all_to_all(dy_out, "expert", 0, 0, tiled=True)

    def by_expert(rows):
        lead = rows.shape[:-2]
        r = rows.reshape((-1, local, cap, rows.shape[-1]))
        return jnp.moveaxis(r, 1, 0).reshape(local, -1, rows.shape[-1])

    def from_expert(rows):
        return jnp.moveaxis(rows.reshape(local, n_expert, cap, rows.shape[-1]), 0, 1).reshape(n_expert, local * cap, rows.shape[-1])

    def d_out_of(xg, dyr):
        g = jnp.sum(xg[..., width : width + 3].astype(F32), -1, keepdims=True)
        return xg[..., :width], (g * dyr.astype(F32)).astype(BF)

    def expert_core(x, d_out, wg, wu, wd):
        eg, eu = mm(x, wg), mm(x, wu)
        act, slope = silu_parts(eg)
        eh = (act * eu).astype(BF)
        d_eh = mm_t(d_out, wd)
        return eh, (d_eh * eu * slope).astype(BF), (d_eh * act).astype(BF)

    xg = by_expert(x_in)
    dyr = by_expert(dy_in)
    outs, dins = [], []
    for i in range(local):
        x, d_out = d_out_of(xg[i], dyr[i])
        eh, d_eg, d_eu = expert_core(x, d_out, expert_gate[i], expert_up[i], expert_down[i])
        outs.append(mm(eh, expert_down[i]).astype(BF))
        dins.append((mm_t(d_eg, expert_gate[i]) + mm_t(d_eu, expert_up[i])).astype(BF))
    ret = from_expert(jnp.concatenate([jnp.stack(outs), jnp.stack(dins)], -1))
    ret = lax.all_to_all(ret, "expert", 0, 0, tiled=True).reshape(slots, 2 * width)

    x_all = by_expert(lax.all_gather(x_in, "context", axis=0, tiled=True))
    dy_all = by_expert(lax.all_gather(dy_in, "context", axis=0, tiled=True))
    rows_all = x_all.shape[1]
    piece = rows_all
    while piece > 1152:
        piece //= 2

    def expert_grads(i):
        def term(carry, k):
            xs = lax.dynamic_slice_in_dim(x_all[i], k * piece, piece, 0)
            ds = lax.dynamic_slice_in_dim(dy_all[i], k * piece, piece, 0)
            x, d_out = d_out_of(xs, ds)
            eh, d_eg, d_eu = expert_core(x, d_out, expert_gate[i], expert_up[i], expert_down[i])
            new = (tmm(x, d_eg), tmm(x, d_eu), tmm(eh, d_out))
            return (new if carry is None else tuple(a + b for a, b in zip(carry, new))), None

        if piece == rows_all:
            return term(None, 0)[0]
        zero = tuple(jnp.zeros(s.shape[1:], F32) for s in (expert_gate, expert_up, expert_down))
        return lax.scan(term, zero, jnp.arange(rows_all // piece))[0]

    eg_grads = [expert_grads(i) for i in range(local)]
    g_expert = tuple(jnp.stack([g[j] for g in eg_grads]) for j in range(3))

    sg, su = mm(nb, shared_gate), mm(nb, shared_up)
    act, slope = silu_parts(sg)
    hs = (act * su).astype(BF)
    shared_out = mm(hs, shared_down)
    d_hs = mm_t(dy, shared_down)
    d_sg = (d_hs * su * slope).astype(BF)
    d_su = (d_hs * act).astype(BF)
    d_b = mm_t(d_sg, shared_gate) + mm_t(d_su, shared_up)

    part = hidden // n_context
    nb_all = lax.all_gather(nb, "context", axis=0, tiled=True)
    dy_seq = lax.all_gather(dy, "context", axis=0, tiled=True)
    wg_s = lax.dynamic_slice_in_dim(shared_gate, me_c * part, part, 1)
    wu_s = lax.dynamic_slice_in_dim(shared_up, me_c * part, part, 1)
    wd_s = lax.dynamic_slice_in_dim(shared_down, me_c * part, part, 0)
    hs_s, dsg_s, dsu_s = expert_core(nb_all, dy_seq, wg_s, wu_s, wd_s)
    gate_s, up_s, down_s = tmm(nb_all, dsg_s), tmm(nb_all, dsu_s), tmm(hs_s, dy_seq)
    rows_of = lambda a: a.astype(BF).reshape(-1, part if a.shape[1] == part else width)
    flat = jnp.concatenate([gate_s.astype(BF).reshape(-1), up_s.astype(BF).reshape(-1), down_s.astype(BF).reshape(-1)]).reshape(n_expert, -1, LANES)
    mine = jnp.sum(lax.all_to_all(flat, "expert", 0, 0, tiled=True).astype(F32), 0).astype(BF)
    whole = lax.all_gather(mine[None], ("context", "expert"), axis=0, tiled=True).reshape(n_context, 3, -1)
    g_sg = jnp.moveaxis(whole[:, 0].reshape(n_context, width, part), 0, 1).reshape(width, hidden).astype(F32)
    g_su = jnp.moveaxis(whole[:, 1].reshape(n_context, width, part), 0, 1).reshape(width, hidden).astype(F32)
    g_sd = whole[:, 2].reshape(hidden, width).astype(F32)

    back_all = [tmm(p, ret) for p in pick_b]
    rows_back = [b[:, :width] for b in back_all]
    moe = gates[:, :1] * rows_back[0] + gates[:, 1:] * rows_back[1]
    result = (h1 + shared_out + moe).astype(BF)
    d_gate = jnp.stack([jnp.sum(dyf * r, -1) for r in rows_back], -1)
    d_chosen = gates * (d_gate - jnp.sum(gates * d_gate, -1, keepdims=True))
    d_logit = jnp.sum(jnp.where(route_hot, d_chosen[..., None], 0.0), 1)
    g_router = lax.dot_general(nb.astype(F32), d_logit, (((0,), (0,)), ((), ())), precision=lax.Precision.HIGHEST)
    d_b = d_b + lax.dot_general(d_logit, w_router.astype(F32), (((1,), (1,)), ((), ())), precision=lax.Precision.HIGHEST)
    d_b = d_b + back_all[0][:, width:] + back_all[1][:, width:]
    g_ffn = jnp.sum(d_b * n_b, 0)
    d_nb = d_b * gain_b
    d_h1 = dyf + rstd_b * (d_nb - n_b * jnp.mean(d_nb * n_b, -1, keepdims=True))
    d_attn = d_h1.astype(BF)
    g_out = tmm(att, d_attn)
    d_att = mm_t(d_attn, w_out).astype(BF)
    delta = jnp.sum(heads_of(d_att.astype(F32) * att_f), -1)

    stats = jnp.concatenate(list(split3(lse)[:2]) + list(split3(delta)[:2]), -1)
    stats = jnp.pad(stats, ((0, 0), (0, LANES - stats.shape[-1])))
    high_d = window(jnp.concatenate([d_attn, stats], -1), down).reshape(nwin * stretch, width + LANES)

    def grads_of(queries, keys, values, d_attended, log_sum, dlt, mask):
        s = jnp.einsum("qhd,khd->hqk", heads_of(queries), heads_of(keys), preferred_element_type=F32) * scale
        p = jnp.where(mask[None], jnp.exp(jnp.where(mask[None], s - log_sum.T[..., None], 0.0)), 0.0)
        dp = jnp.einsum("qhd,khd->hqk", heads_of(d_attended), heads_of(values), preferred_element_type=F32)
        return p.astype(BF), (p * (dp - dlt.T[..., None])).astype(BF)

    _, ds = grads_of(q, kw, vw, d_att, lse, delta, allowed)
    d_q = scale * jnp.einsum("hqk,khd->qhd", ds, heads_of(kw), preferred_element_type=F32).reshape(stretch, width)
    own_rope = rope_table(own_pos)
    d_q_pre = rotate(d_q, *own_rope, -1.0).astype(BF)

    high_q = rotate(mm(norm_in(high_tok), w_query), *rope_table(high_pos), 1.0).astype(BF)
    st = high_d[:, width:].astype(F32)
    high_lse = st[:, :HEADS] + st[:, HEADS : 2 * HEADS]
    high_delta = st[:, 2 * HEADS : 3 * HEADS] + st[:, 3 * HEADS : 4 * HEADS]
    high_datt = mm_t(high_d[:, :width], w_out).astype(BF)
    mask = (high_seg[:, None] == seg[None, :]) & (own_pos[None, :] <= high_pos[:, None]) & (high_pos[:, None] < n_context * stretch)
    k_own, v_own = kw[:stretch], vw[:stretch]
    p2, ds2 = grads_of(high_q, k_own, v_own, high_datt, high_lse, high_delta, mask)
    d_k = scale * jnp.einsum("hqk,qhd->khd", ds2, heads_of(high_q), preferred_element_type=F32).reshape(stretch, width)
    d_v = jnp.einsum("hqk,qhd->khd", p2, heads_of(high_datt), preferred_element_type=F32).reshape(stretch, width)
    d_k_pre = rotate(d_k, *own_rope, -1.0).astype(BF)
    d_v_low = d_v.astype(BF)
    g_q, g_k, g_v = tmm(na, d_q_pre), tmm(na, d_k_pre), tmm(na, d_v_low)
    d_a = mm_t(d_q_pre, w_query) + mm_t(d_k_pre, w_key) + mm_t(d_v_low, w_value)
    rstd_a = lax.rsqrt(jnp.mean(tokf * tokf, -1, keepdims=True) + EPSILON)
    n_a = tokf * rstd_a
    g_attn = jnp.sum(d_a * n_a, 0)
    d_na = d_a * gain_a
    d_tokens = d_h1 + rstd_a * (d_na - n_a * jnp.mean(d_na * n_a, -1, keepdims=True))

    def scatter(x, axis, groups, n):
        parts = x.reshape((n, x.shape[0] // n) + x.shape[1:])
        got = lax.all_to_all(parts, axis, 0, 0, axis_index_groups=groups, tiled=True)
        return jnp.sum(got.astype(F32), 0).astype(BF)

    def spread(x, axis, groups, n):
        parts = jnp.broadcast_to(x[None], (n,) + x.shape)
        got = lax.all_to_all(parts, axis, 0, 0, axis_index_groups=groups, tiled=True)
        return got.reshape((n * x.shape[0],) + x.shape[1:])

    def reduce_all(x):
        x = scatter(x, "context", pair_groups, 2)
        x = scatter(x, "expert", None, n_expert)
        x = scatter(x, "context", chip_groups, chips)
        x = spread(x, "context", chip_groups, chips)
        x = spread(x, "expert", None, n_expert)
        return spread(x, "context", pair_groups, 2)

    small = jnp.concatenate([g_attn[None], g_ffn[None], g_router.T], 0)
    small = jnp.pad(small, ((0, 256 - small.shape[0]), (0, 0)))
    first = reduce_all(g_out.astype(BF)).astype(F32)
    last = reduce_all(jnp.concatenate([g_q, g_k, g_v, small], 0).astype(BF)).astype(F32)
    g_q, g_k, g_v, small = last[:width], last[width : 2 * width], last[2 * width : 3 * width], last[3 * width :]
    return (
        result[None], d_tokens[None], small[0], g_q, g_k, g_v, first, small[1],
        small[2 : 2 + experts].T, g_sg, g_su, g_sd, g_expert[0], g_expert[1], g_expert[2],
    )


def solution(mesh):
    rows = P("expert", "context", None)
    owned = P("expert", None, None)
    placed = (rows, P("expert", "context"), rows) + (P(),) * 10 + (owned,) * 3 + (rows,)
    return jax.shard_map(
        per_device, mesh=mesh, in_specs=placed,
        out_specs=(rows, rows) + (P(),) * 10 + (owned,) * 3, check_vma=False,
    )
```

```python
import functools
import math

import jax
import jax.numpy as jnp
from jax import lax
from jax.experimental import pallas as pl
from jax.experimental.pallas import tpu as pltpu
from jax.sharding import PartitionSpec as P

HEADS = 12
HEAD = 64
TOP = 2
EPSILON = 1e-06
MASKED = -1e30
LANES = 128
GROUP = 4
TILE = GROUP * HEAD
BF = jnp.bfloat16
F32 = jnp.float32
HIGHEST = lax.Precision.HIGHEST


def mm(a, b, **k):
    return jnp.dot(a, b, preferred_element_type=F32, **k)


def mm_t(a, b, **k):
    return lax.dot_general(a, b, (((1,), (1,)), ((), ())), preferred_element_type=F32, **k)


def tmm(a, b, **k):
    return lax.dot_general(a, b, (((0,), (0,)), ((), ())), preferred_element_type=F32, **k)


def silu_parts(v):
    s = 1.0 / (1.0 + jnp.exp(-v))
    act = v * s
    return act, s + act * (1.0 - s)


def silu_grads(gate, up, d_hidden):
    act, slope = silu_parts(gate)
    return (act * up).astype(BF), (d_hidden * up * slope).astype(BF), (d_hidden * act).astype(BF)


def split_bf(v, n):
    parts = []
    for _ in range(n):
        p = v.astype(BF)
        parts.append(p)
        v = v - p.astype(F32)
    return parts


def norm_rows(x):
    r = lax.rsqrt(jnp.mean(x * x, -1, keepdims=True) + EPSILON)
    return x * r, r


def turn(x, cos, sin, sign):
    lane = lax.broadcasted_iota(jnp.int32, x.shape, 1)
    half = HEAD // 2
    other = jnp.where(lane % HEAD < half, pltpu.roll(x, TILE - half, 1), pltpu.roll(x, half, 1))
    reps = TILE // LANES
    return x * jnp.concatenate([cos] * reps, 1) + sign * other * jnp.concatenate([sin] * reps, 1)


def by_head(x):
    lane = lax.broadcasted_iota(jnp.int32, x.shape, 1) // HEAD
    return jnp.concatenate([jnp.where(lane == h, x, jnp.zeros_like(x)) for h in range(GROUP)], 0)


def from_head(x, rows):
    lane = lax.broadcasted_iota(jnp.int32, (rows, TILE), 1) // HEAD
    out = x[:rows]
    for h in range(1, GROUP):
        out = jnp.where(lane == h, x[h * rows : (h + 1) * rows], out)
    return out


def column(stats, j):
    lane = lax.broadcasted_iota(jnp.int32, stats.shape, 1)
    return jnp.concatenate([jnp.sum(jnp.where(lane == GROUP * j + h, stats, 0.0), -1, keepdims=True) for h in range(GROUP)], 0)


def seg_row(win, blocks, stretch):
    return jnp.concatenate([win[b, stretch : stretch + 1, :stretch].astype(F32) for b in range(blocks)], 1)


def win_rows(win, blocks, stretch):
    return jnp.concatenate([win[b, :stretch, :] for b in range(blocks)], 0)


def whole_spec(shape):
    return pl.BlockSpec(shape, lambda *_: (0,) * len(shape))


def call(kernel, grid, in_specs, out_specs, out_shape, scratch=(), flops=0, nbytes=0, name=None, aliases=None):
    return pl.pallas_call(
        kernel, grid=grid, in_specs=in_specs, out_specs=out_specs, out_shape=out_shape,
        scratch_shapes=list(scratch), name=name, input_output_aliases=aliases or {},
        compiler_params=pltpu.CompilerParams(dimension_semantics=("arbitrary",) * len(grid), vmem_limit_bytes=60 << 20),
        cost_estimate=pl.CostEstimate(flops=flops, bytes_accessed=nbytes, transcendentals=0),
    )


def sds(shape, dtype):
    return jax.ShapeDtypeStruct(shape, dtype)


def forward_body(stretch, win_blocks, win, own_seg, own_pos, low_pos, cos, sin, gain_a, gain_b, wq, wk, wv, wo, wr, hot0, hot1, pick0, pick1,
                 na_out, q_out, k_out, v_out, att_out, attb_out, lse_out, h1_out, nb_out, gates_out, send_out, na_all):
    j = pl.program_id(0)
    rows = stretch

    @pl.when(j == 0)
    def _():
        for b in range(win_blocks):
            x = win[b, :stretch, :].astype(F32)
            na_all[b * stretch : (b + 1) * stretch, :] = (norm_rows(x)[0] * gain_a[...]).astype(BF)
        na_out[...] = na_all[:rows, :]
        h1_out[...] = win[0, :stretch, :].astype(F32)
        lse_out[...] = jnp.zeros_like(lse_out)

    own = na_all[:rows, :]
    q = turn(mm(own, wq[...]), cos[:rows, :], sin[:rows, :], 1.0).astype(BF)
    k = turn(mm(na_all[...], wk[...]), cos[...], sin[...], 1.0).astype(BF)
    v = mm(na_all[...], wv[...]).astype(BF)
    q_out[...] = q
    k_out[...] = k
    v_out[...] = v
    s = mm_t(by_head(q), k) * (HEAD ** -0.5)
    allowed = (own_seg[...] == seg_row(win, win_blocks, stretch)) & (low_pos[...] <= own_pos[...]) & (low_pos[...] >= 0)
    allowed = jnp.concatenate([allowed] * GROUP, 0)
    s = jnp.where(allowed, s, MASKED)
    peak = jnp.max(s, -1, keepdims=True)
    e = jnp.where(allowed, jnp.exp(s - peak), 0.0)
    total = jnp.sum(e, -1, keepdims=True)
    att = from_head(mm(e.astype(BF), v) / total, rows)
    lse = peak + jnp.log(total)
    lane = lax.broadcasted_iota(jnp.int32, (rows, LANES), 1)
    stat = lse_out[...]
    for h in range(GROUP):
        stat = jnp.where(lane == GROUP * j + h, lse[h * rows : (h + 1) * rows], stat)
    lse_out[...] = stat
    att_out[...] = att
    attb_out[...] = att.astype(BF)
    h1_out[...] += mm(att.astype(BF), wo[...])

    @pl.when(j == pl.num_programs(0) - 1)
    def _():
        n_b, _ = norm_rows(h1_out[...])
        nb = (n_b * gain_b[...]).astype(BF)
        nb_out[...] = nb
        logits = mm(nb, wr[...])
        l0 = jnp.sum(logits * hot0[...].astype(F32), -1, keepdims=True)
        l1 = jnp.sum(logits * hot1[...].astype(F32), -1, keepdims=True)
        top = jnp.maximum(l0, l1)
        e0, e1 = jnp.exp(l0 - top), jnp.exp(l1 - top)
        g0, g1 = e0 / (e0 + e1), e1 / (e0 + e1)
        gates_out[...] = jnp.where(lane == 0, g0, jnp.where(lane == 1, g1, 0.0))
        width = nb.shape[1]
        send_out[:, :width] = mm(pick0[...] + pick1[...], nb).astype(BF)
        part = []
        for g in (g0, g1):
            a, b, c = split_bf(g, 3)
            part.append(jnp.where(lane == 0, a.astype(F32), jnp.where(lane == 1, b.astype(F32), jnp.where(lane == 2, c.astype(F32), 0.0))).astype(BF))
        send_out[:, width:] = (mm(pick0[...], part[0]) + mm(pick1[...], part[1])).astype(BF)


def forward(win, own_seg, own_pos, low_pos, cos, sin, gain_a, gain_b, wq, wk, wv, wo, wr, hot0, hot1, pick0, pick1):
    blocks, packet, width = win.shape
    stretch = own_seg.shape[0]
    n = blocks * stretch
    slots = pick0.shape[0]
    wide = lambda r: pl.BlockSpec((r, TILE), lambda j: (0, j))
    tall = pl.BlockSpec((TILE, width), lambda j: (j, 0))
    full = lambda a: whole_spec(a.shape)
    shapes = [((stretch, width), BF), ((stretch, width), BF), ((n, width), BF), ((n, width), BF), ((stretch, width), F32), ((stretch, width), BF),
              ((stretch, LANES), F32), ((stretch, width), F32), ((stretch, width), BF), ((stretch, LANES), F32), ((slots, width + LANES), BF)]
    specs = [whole_spec((stretch, width)), wide(stretch), wide(n), wide(n), wide(stretch), wide(stretch)] + [whole_spec(s) for s, _ in shapes[6:]]
    return call(
        functools.partial(forward_body, stretch, blocks), (width // TILE,),
        [full(win), full(own_seg), full(own_pos), full(low_pos), full(cos), full(sin), full(gain_a), full(gain_b), wide(width), wide(width), wide(width), tall,
         full(wr), full(hot0), full(hot1), full(pick0), full(pick1)],
        specs, [sds(s, d) for s, d in shapes], [pltpu.VMEM((n, width), BF)],
        flops=4 * n * width * width, nbytes=12 * width * width, name="attention_forward",
    )(win, own_seg, own_pos, low_pos, cos, sin, gain_a, gain_b, wq, wk, wv, wo, wr, hot0, hot1, pick0, pick1)


def shared_body(nb, dy, wg, wu, wd, out, d_b):
    j = pl.program_id(0)
    hs, d_sg, d_su = silu_grads(mm(nb[...], wg[...]), mm(nb[...], wu[...]), mm_t(dy[...], wd[...]))
    o = mm(hs, wd[...])
    d = mm_t(d_sg, wg[...]) + mm_t(d_su, wu[...])

    @pl.when(j == 0)
    def _():
        out[...] = o
        d_b[...] = d

    @pl.when(j > 0)
    def _():
        out[...] += o
        d_b[...] += d


def shared(nb, dy, wg, wu, wd):
    rows, width = nb.shape
    hidden = wg.shape[1]
    tile = 512
    wide = pl.BlockSpec((width, tile), lambda j: (0, j))
    return call(
        shared_body, (hidden // tile,),
        [whole_spec(nb.shape), whole_spec(dy.shape), wide, wide, pl.BlockSpec((tile, width), lambda j: (j, 0))],
        [whole_spec((rows, width))] * 2, [sds((rows, width), F32)] * 2,
        flops=12 * rows * width * hidden, nbytes=6 * width * hidden, name="shared_branch",
    )(nb, dy, wg, wu, wd)


def gated(xg, dyr, width):
    g = jnp.sum(xg[:, width:].astype(F32), -1, keepdims=True)
    return (g * dyr.astype(F32)).astype(BF)


def experts_body(xg, dyr, wg, wu, wd, ret, o_acc, d_acc, d_out):
    j = pl.program_id(1)
    width = dyr.shape[2]

    @pl.when(j == 0)
    def _():
        d_out[...] = gated(xg[0], dyr[0], width)
        o_acc[...] = jnp.zeros_like(o_acc)
        d_acc[...] = jnp.zeros_like(d_acc)

    x = xg[0, :, :width]
    eh, d_eg, d_eu = silu_grads(mm(x, wg[0]), mm(x, wu[0]), mm_t(d_out[...], wd[0]))
    o_acc[...] += mm(eh, wd[0])
    d_acc[...] += mm_t(d_eg, wg[0]) + mm_t(d_eu, wu[0])

    @pl.when(j == pl.num_programs(1) - 1)
    def _():
        ret[0, :, :width] = o_acc[...].astype(BF)
        ret[0, :, width:] = d_acc[...].astype(BF)


def experts_visit(xg, dyr, wg, wu, wd):
    local, rows, width = dyr.shape
    hidden = wg.shape[2]
    tile = 512
    wide = pl.BlockSpec((1, width, tile), lambda i, j: (i, 0, j))
    return call(
        experts_body, (local, hidden // tile),
        [pl.BlockSpec((1,) + xg.shape[1:], lambda i, j: (i, 0, 0)), pl.BlockSpec((1,) + dyr.shape[1:], lambda i, j: (i, 0, 0)), wide, wide,
         pl.BlockSpec((1, tile, width), lambda i, j: (i, j, 0))],
        pl.BlockSpec((1, rows, 2 * width), lambda i, j: (i, 0, 0)), sds((local, rows, 2 * width), BF),
        [pltpu.VMEM((rows, width), F32), pltpu.VMEM((rows, width), F32), pltpu.VMEM((rows, width), BF)],
        flops=12 * local * rows * width * hidden, nbytes=6 * local * width * hidden, name="experts_visit",
    )(xg, dyr, wg, wu, wd)


def expert_grads_body(piece, xg, dyr, wg, wu, wd, g_gate, g_up, g_down, x_all, d_out):
    j = pl.program_id(1)
    groups, _, per, width = dyr.shape

    @pl.when(j == 0)
    def _():
        for c in range(groups):
            x_all[c * per : (c + 1) * per, :] = xg[c, 0, :, :width]
            d_out[c * per : (c + 1) * per, :] = gated(xg[c, 0], dyr[c, 0], width)

    rows = groups * per
    for n in range(rows // piece):
        x, d = x_all[n * piece : (n + 1) * piece, :], d_out[n * piece : (n + 1) * piece, :]
        eh, d_eg, d_eu = silu_grads(mm(x, wg[0]), mm(x, wu[0]), mm_t(d, wd[0]))
        terms = (tmm(x, d_eg), tmm(x, d_eu), tmm(eh, d))
        for ref, term in zip((g_gate, g_up, g_down), terms):
            ref[0] = term if n == 0 else ref[0] + term


def expert_grads(xg, dyr, wg, wu, wd):
    groups, local, per, width = dyr.shape
    hidden = wg.shape[2]
    rows = groups * per
    piece = rows
    while piece > 1152:
        piece //= 2
    tile = 256
    wide = pl.BlockSpec((1, width, tile), lambda i, j: (i, 0, j))
    tall = pl.BlockSpec((1, tile, width), lambda i, j: (i, j, 0))
    return call(
        functools.partial(expert_grads_body, piece), (local, hidden // tile),
        [pl.BlockSpec((groups, 1) + xg.shape[2:], lambda i, j: (0, i, 0, 0)), pl.BlockSpec((groups, 1) + dyr.shape[2:], lambda i, j: (0, i, 0, 0)), wide, wide, tall],
        [wide, wide, tall], [sds(wg.shape, F32), sds(wu.shape, F32), sds(wd.shape, F32)],
        [pltpu.VMEM((rows, width), BF), pltpu.VMEM((rows, width), BF)],
        flops=12 * local * rows * width * hidden, nbytes=18 * local * width * hidden, name="expert_grads",
    )(xg, dyr, wg, wu, wd)


def combine_body(experts, ret, pick0, pick1, gates, h1, shared_out, d_b_in, dy, nb, gain_b, wr, hot0, hot1, att, attb, lse, wo,
                 result, d_h1_out, pack, datt_out, delta_out, g_out, small):
    width = dy.shape[1]
    g0, g1 = gates[:, 0:1], gates[:, 1:2]
    back0, back1 = tmm(pick0[...], ret[...]), tmm(pick1[...], ret[...])
    dyf = dy[...].astype(F32)
    result[...] = (h1[...] + shared_out[...] + (g0 * back0[:, :width] + g1 * back1[:, :width])).astype(BF)
    dg0 = jnp.sum(dyf * back0[:, :width], -1, keepdims=True)
    dg1 = jnp.sum(dyf * back1[:, :width], -1, keepdims=True)
    mean = g0 * dg0 + g1 * dg1
    d_logit = hot0[...].astype(F32) * (g0 * (dg0 - mean)) + hot1[...].astype(F32) * (g1 * (dg1 - mean))
    d_b = d_b_in[...] + mm_t(d_logit, wr[...].astype(F32), precision=HIGHEST) + back0[:, width:] + back1[:, width:]
    n_b, r = norm_rows(h1[...])
    d_nb = d_b * gain_b[...]
    d_h1 = dyf + r * (d_nb - n_b * jnp.mean(d_nb * n_b, -1, keepdims=True))
    d_h1_out[...] = d_h1
    d_attn = d_h1.astype(BF)
    datt = mm_t(d_attn, wo[...]).astype(BF)
    datt_out[...] = datt
    head_of = (lax.broadcasted_iota(jnp.int32, (width, LANES), 0) // HEAD == lax.broadcasted_iota(jnp.int32, (width, LANES), 1)).astype(F32)
    delta = mm(datt.astype(F32) * att[...], head_of, precision=HIGHEST)
    delta_out[...] = delta
    parts = [p.astype(F32) for p in split_bf(lse[...], 2) + split_bf(delta, 2)]
    packed = parts[0]
    for n in range(1, 4):
        packed = packed + pltpu.roll(parts[n], 16 * n, 1)
    pack[:, :width] = d_attn
    pack[:, width:] = packed.astype(BF)
    g_out[...] = tmm(attb[...], d_attn).astype(BF)
    router = tmm(d_logit, nb[...].astype(F32), precision=HIGHEST)
    small[...] = jnp.zeros_like(small)
    small[0:1, :] = jnp.sum(d_b * n_b, 0, keepdims=True)
    small[8 : 8 + experts, :] = router[:experts]


def combine(experts, ret, pick0, pick1, gates, h1, shared_out, d_b, dy, nb, gain_b, wr, hot0, hot1, att, attb, lse, wo):
    rows, width = dy.shape
    args = (ret, pick0, pick1, gates, h1, shared_out, d_b, dy, nb, gain_b, wr, hot0, hot1, att, attb, lse, wo)
    shapes = [((rows, width), BF), ((rows, width), F32), ((rows, width + LANES), BF), ((rows, width), BF), ((rows, LANES), F32), ((width, width), BF), ((32, width), F32)]
    return call(
        functools.partial(combine_body, experts), (1,), [whole_spec(a.shape) for a in args],
        [whole_spec(s) for s, _ in shapes], [sds(s, d) for s, d in shapes],
        flops=8 * rows * width * width, nbytes=8 * width * width, name="combine",
    )(*args)


def d_query_body(stretch, win_blocks, win, own_seg, own_pos, low_pos, cos, sin, q, k, v, datt, lse, delta, na, wq, g_q, d_a):
    j = pl.program_id(0)
    allowed = (own_seg[...] == seg_row(win, win_blocks, stretch)) & (low_pos[...] <= own_pos[...]) & (low_pos[...] >= 0)
    allowed = jnp.concatenate([allowed] * GROUP, 0)
    s = mm_t(by_head(q[...]), k[...]) * (HEAD ** -0.5)
    p = jnp.where(allowed, jnp.exp(jnp.where(allowed, s - column(lse[...], j), 0.0)), 0.0)
    dp = mm_t(by_head(datt[...]), v[...])
    ds = (p * (dp - column(delta[...], j))).astype(BF)
    dq = from_head(mm(ds, k[...]), stretch) * (HEAD ** -0.5)
    dq = turn(dq, cos[:stretch, :], sin[:stretch, :], -1.0).astype(BF)
    g_q[...] = tmm(na[...], dq).astype(BF)
    d = mm_t(dq, wq[...])

    @pl.when(j == 0)
    def _():
        d_a[...] = d

    @pl.when(j > 0)
    def _():
        d_a[...] += d


def d_query(win, own_seg, own_pos, low_pos, cos, sin, q, k, v, datt, lse, delta, na, wq):
    blocks, _, width = win.shape
    stretch = own_seg.shape[0]
    n = blocks * stretch
    wide = lambda r: pl.BlockSpec((r, TILE), lambda j: (0, j))
    full = lambda a: whole_spec(a.shape)
    return call(
        functools.partial(d_query_body, stretch, blocks), (width // TILE,),
        [full(win), full(own_seg), full(own_pos), full(low_pos), full(cos), full(sin), wide(stretch), wide(n), wide(n), wide(stretch), full(lse), full(delta), full(na), wide(width)],
        [wide(width), whole_spec((stretch, width))], [sds((width, width), BF), sds((stretch, width), F32)],
        flops=24 * stretch * n * width, nbytes=8 * n * width, name="attention_d_query",
    )(win, own_seg, own_pos, low_pos, cos, sin, q, k, v, datt, lse, delta, na, wq)


def d_key_body(stretch, win_blocks, limit, win, pack, own_seg, own_pos, high_pos, cos, sin, k, v, na, wq, wk, wv, wo, d_a_in, d_h1, gain_a,
               g_k, g_v, d_tokens, g_attn, na_all, stat, d_a):
    j = pl.program_id(0)
    width = na.shape[1]

    @pl.when(j == 0)
    def _():
        for b in range(win_blocks):
            x = win[b, :stretch, :].astype(F32)
            na_all[b * stretch : (b + 1) * stretch, :] = (norm_rows(x)[0] * gain_a[...]).astype(BF)
            st = pack[b, :, width:].astype(F32)
            st = st + pltpu.roll(st, LANES - 16, 1)
            stat[:, b * stretch : (b + 1) * stretch] = st.T
        d_a[...] = d_a_in[...]

    q = turn(mm(na_all[...], wq[...]), cos[...], sin[...], 1.0).astype(BF)
    datt = jnp.concatenate([mm_t(pack[b, :, :width], wo[...]).astype(BF) for b in range(win_blocks)], 0)
    allowed = (own_seg[...] == seg_row(win, win_blocks, stretch)) & (own_pos[...] <= high_pos[...]) & (high_pos[...] < limit)
    allowed = jnp.concatenate([allowed] * GROUP, 0)
    n = win_blocks * stretch
    lse = jnp.concatenate([jnp.broadcast_to(stat[pl.ds(GROUP * j + h, 1), :], (stretch, n)) for h in range(GROUP)], 0)
    delta = jnp.concatenate([jnp.broadcast_to(stat[pl.ds(32 + GROUP * j + h, 1), :], (stretch, n)) for h in range(GROUP)], 0)
    s = mm_t(by_head(k[...]), q) * (HEAD ** -0.5)
    p = jnp.where(allowed, jnp.exp(jnp.where(allowed, s - lse, 0.0)), 0.0)
    dp = mm_t(by_head(v[...]), datt)
    ds = (p * (dp - delta)).astype(BF)
    dk = from_head(mm(ds, q), stretch) * (HEAD ** -0.5)
    dk = turn(dk, cos[:stretch, :], sin[:stretch, :], -1.0).astype(BF)
    dv = from_head(mm(p.astype(BF), datt), stretch).astype(BF)
    g_k[...] = tmm(na[...], dk).astype(BF)
    g_v[...] = tmm(na[...], dv).astype(BF)
    d_a[...] += mm_t(dk, wk[...]) + mm_t(dv, wv[...])

    @pl.when(j == pl.num_programs(0) - 1)
    def _():
        n_a, r = norm_rows(win[0, :stretch, :].astype(F32))
        total = d_a[...]
        g_attn[...] = jnp.sum(total * n_a, 0, keepdims=True)
        d_na = total * gain_a[...]
        d_tokens[...] = d_h1[...] + r * (d_na - n_a * jnp.mean(d_na * n_a, -1, keepdims=True))


def d_key(limit, win, pack, own_seg, own_pos, high_pos, cos, sin, k, v, na, wq, wk, wv, wo, d_a, d_h1, gain_a):
    blocks, _, width = win.shape
    stretch = own_seg.shape[0]
    n = blocks * stretch
    wide = lambda r: pl.BlockSpec((r, TILE), lambda j: (0, j))
    tall = pl.BlockSpec((TILE, width), lambda j: (j, 0))
    full = lambda a: whole_spec(a.shape)
    return call(
        functools.partial(d_key_body, stretch, blocks, limit), (width // TILE,),
        [full(win), full(pack), full(own_seg), full(own_pos), full(high_pos), full(cos), full(sin), wide(stretch), wide(stretch), full(na), wide(width), wide(width), wide(width), tall,
         full(d_a), full(d_h1), full(gain_a)],
        [wide(width), wide(width), whole_spec((stretch, width)), whole_spec((1, width))],
        [sds((width, width), BF), sds((width, width), BF), sds((stretch, width), F32), sds((1, width), F32)],
        [pltpu.VMEM((n, width), BF), pltpu.VMEM((LANES, n), F32), pltpu.VMEM((stretch, width), F32)],
        flops=24 * stretch * n * width + 4 * n * width * width, nbytes=8 * n * width, name="attention_d_key",
    )(win, pack, own_seg, own_pos, high_pos, cos, sin, k, v, na, wq, wk, wv, wo, d_a, d_h1, gain_a)


def shared_grads_body(me, nb, dy, wg, wu, wd, out):
    width = nb.shape[1]
    part = wg.shape[1]
    hs, d_sg, d_su = silu_grads(mm(nb[...], wg[...]), mm(nb[...], wu[...]), mm_t(dy[...], wd[...]))
    at = 0
    for d in (d_sg, d_su):
        g = tmm(nb[...], d).astype(BF)
        for n in range(part // LANES):
            out[at : at + width, :] = g[:, n * LANES : (n + 1) * LANES]
            at += width
    g = tmm(hs, dy[...]).astype(BF)
    for n in range(width // LANES):
        out[at : at + part, :] = g[:, n * LANES : (n + 1) * LANES]
        at += part


def shared_grads(me, nb, dy, wg, wu, wd, part):
    rows, width = nb.shape
    total = 3 * width * part // LANES
    wide = pl.BlockSpec((width, part), lambda i, me: (0, me[0]))
    return pl.pallas_call(
        shared_grads_body,
        grid_spec=pltpu.PrefetchScalarGridSpec(
            num_scalar_prefetch=1, grid=(1,),
            in_specs=[whole_spec(nb.shape), whole_spec(dy.shape), wide, wide, pl.BlockSpec((part, width), lambda i, me: (me[0], 0))],
            out_specs=whole_spec((total, LANES)),
        ),
        out_shape=sds((total, LANES), BF), name="shared_grads",
        compiler_params=pltpu.CompilerParams(vmem_limit_bytes=60 << 20),
        cost_estimate=pl.CostEstimate(flops=12 * rows * width * part, bytes_accessed=4 * rows * width, transcendentals=0),
    )(me, nb, dy, wg, wu, wd)


def place_body(part, parts, gate, up, down):
    width = gate.shape[0]
    at = 0
    for ref in (gate, up):
        for n in range(part // LANES):
            ref[:, n * LANES : (n + 1) * LANES] = parts[0, at : at + width, :].astype(F32)
            at += width
    for n in range(width // LANES):
        down[:, n * LANES : (n + 1) * LANES] = parts[0, at : at + part, :].astype(F32)
        at += part


def place_shared(parts, width, part):
    count, total, _ = parts.shape
    wide = pl.BlockSpec((width, part), lambda c: (0, c))
    return call(
        functools.partial(place_body, part), (count,), [pl.BlockSpec((1, total, LANES), lambda c: (c, 0, 0))],
        [wide, wide, pl.BlockSpec((part, width), lambda c: (c, 0))],
        [sds((width, part * count), F32), sds((width, part * count), F32), sds((part * count, width), F32)],
        nbytes=6 * parts.size, name="place_shared_grads",
    )(parts)


def per_device(
    tokens, segments, routes, attn_gain, w_query, w_key, w_value, w_out, ffn_gain, w_router,
    shared_gate, shared_up, shared_down, expert_gate, expert_up, expert_down, cotangent,
):
    _, stretch, width = tokens.shape
    n_expert = lax.axis_size("expert")
    n_context = lax.axis_size("context")
    chips = n_context // 2
    back = n_context // 4
    me_c = lax.axis_index("context")
    local = expert_gate.shape[0]
    experts = n_expert * local
    cap = (9 * stretch * TOP + 8 * experts - 1) // (8 * experts)
    slots = experts * cap
    hidden = shared_gate.shape[1]
    part = hidden // n_context
    pair_groups = [[2 * i, 2 * i + 1] for i in range(chips)]
    chip_groups = [[2 * i + k for i in range(chips)] for k in range(2)]
    swap = [(c, c ^ 1) for c in range(n_context)]

    def up(d):
        return [(c, c + 2 * d) for c in range(n_context - 2 * d)]

    def down(d):
        return [(c + 2 * d, c) for c in range(n_context - 2 * d)]

    def window(block, steps):
        mine = jnp.stack([block] + [lax.ppermute(block, "context", steps(d)) for d in range(1, back + 1)])
        other = lax.ppermute(mine, "context", swap)
        return jnp.concatenate([mine, other], 0)

    def window_pos(sign):
        d = 2 * sign * jnp.arange(back + 1, dtype=jnp.int32)
        blocks = jnp.concatenate([me_c + d, (me_c ^ 1) + d])
        return (blocks[:, None] * stretch + jnp.arange(stretch, dtype=jnp.int32)[None, :]).reshape(1, -1)

    def rope_table(positions):
        half = HEAD // 2
        frequency = jnp.exp(jnp.arange(half, dtype=F32) * (-2.0 * math.log(10000.0) / HEAD))
        angles = positions.reshape(-1).astype(F32)[:, None] * frequency[None, :]
        c, s = jnp.cos(angles), jnp.sin(angles)
        return jnp.concatenate([c] * 4, 1), jnp.concatenate([-s, s] * 2, 1)

    tok, dy = tokens[0], cotangent[0]
    packet = jnp.concatenate([tok, jnp.pad(segments.astype(BF), ((0, 7), (0, width - stretch)))], 0)
    low_win = window(packet, up)
    high_win = window(packet, down)
    own_seg = segments[0].astype(F32)[:, None]
    own_pos = (me_c * stretch + jnp.arange(stretch, dtype=jnp.int32))[:, None]
    low_pos, high_pos = window_pos(-1), window_pos(1)
    low_cos, low_sin = rope_table(low_pos)
    high_cos, high_sin = rope_table(high_pos)
    gain_a, gain_b = attn_gain.astype(F32)[None], ffn_gain.astype(F32)[None]

    assigned = routes[0].reshape(stretch * TOP)
    onehot = assigned[:, None] == jnp.arange(experts, dtype=jnp.int32)[None, :]
    row_i = jnp.arange(stretch * TOP, dtype=jnp.int32)
    before = mm((row_i[:, None] > row_i[None, :]).astype(BF), onehot.astype(BF))
    place = jnp.sum(jnp.where(onehot, before, 0.0), -1).astype(jnp.int32)
    slot = jnp.where(place < cap, assigned * cap + place, slots).reshape(stretch, TOP)
    slot_i = jnp.arange(slots, dtype=jnp.int32)
    pick0, pick1 = [(slot_i[:, None] == slot[None, :, r]).astype(BF) for r in range(TOP)]
    lane_i = jnp.arange(LANES, dtype=jnp.int32)
    hot0, hot1 = [(routes[0][:, r : r + 1] == lane_i[None, :]).astype(BF) for r in range(TOP)]
    router = jnp.pad(w_router, ((0, 0), (0, LANES - experts)))

    def exchange(rows):
        got = lax.all_to_all(rows.reshape(n_expert, local * cap, rows.shape[-1]), "expert", 0, 0, tiled=True)
        return jnp.moveaxis(got.reshape(n_expert, local, cap, rows.shape[-1]), 1, 0).reshape(local, n_expert * cap, rows.shape[-1])

    dy_in = exchange(mm(pick0 + pick1, dy).astype(BF))
    na, q, k, v, att, attb, lse, h1, nb, gates, send = forward(
        low_win, own_seg, own_pos, low_pos, low_cos, low_sin, gain_a, gain_b, w_query, w_key, w_value, w_out, router, hot0, hot1, pick0, pick1
    )
    x_in = exchange(send)
    ret = experts_visit(x_in, dy_in, expert_gate, expert_up, expert_down)
    ret = jnp.moveaxis(ret.reshape(local, n_expert, cap, 2 * width), 0, 1).reshape(n_expert, local * cap, 2 * width)
    ret = lax.all_to_all(ret, "expert", 0, 0, tiled=True).reshape(slots, 2 * width)
    x_all = lax.all_gather(x_in, "context", axis=0)
    dy_all = lax.all_gather(dy_in, "context", axis=0)
    g_eg, g_eu, g_ed = expert_grads(x_all, dy_all, expert_gate, expert_up, expert_down)

    shared_out, d_b = shared(nb, dy, shared_gate, shared_up, shared_down)
    nb_all = lax.all_gather(nb, "context", axis=0, tiled=True)
    dy_seq = lax.all_gather(dy, "context", axis=0, tiled=True)
    if part % LANES == 0:
        flat = shared_grads(me_c.reshape(1).astype(jnp.int32), nb_all, dy_seq, shared_gate, shared_up, shared_down, part)
    else:
        own_gate = lax.dynamic_slice_in_dim(shared_gate, me_c * part, part, 1)
        own_up = lax.dynamic_slice_in_dim(shared_up, me_c * part, part, 1)
        own_down = lax.dynamic_slice_in_dim(shared_down, me_c * part, part, 0)
        hs, d_sg, d_su = silu_grads(mm(nb_all, own_gate), mm(nb_all, own_up), mm_t(dy_seq, own_down))
        flat = jnp.concatenate([tmm(nb_all, d_sg).astype(BF).reshape(-1), tmm(nb_all, d_su).astype(BF).reshape(-1), tmm(hs, dy_seq).astype(BF).reshape(-1)])
    flat = flat.reshape(n_expert, -1, LANES)
    mine = jnp.sum(lax.all_to_all(flat, "expert", 0, 0, tiled=True).astype(F32), 0).astype(BF)
    whole = lax.all_gather(mine, ("context", "expert"), axis=0, tiled=True)
    if part % LANES == 0:
        g_sg, g_su, g_sd = place_shared(whole.reshape(n_context, -1, LANES), width, part)
    else:
        whole = whole.reshape(n_context, 3, -1)
        g_sg, g_su = [jnp.moveaxis(whole[:, n].reshape(n_context, width, part), 0, 1).reshape(width, hidden).astype(F32) for n in range(2)]
        g_sd = whole[:, 2].reshape(hidden, width).astype(F32)

    result, d_h1, pack, datt, delta, g_out, small = combine(
        experts, ret, pick0, pick1, gates, h1, shared_out, d_b, dy, nb, gain_b, router, hot0, hot1, att, attb, lse, w_out
    )
    high_pack = window(pack, down)
    g_q, d_a = d_query(low_win, own_seg, own_pos, low_pos, low_cos, low_sin, q, k, v, datt, lse, delta, na, w_query)
    g_k, g_v, d_tokens, g_attn = d_key(
        n_context * stretch, high_win, high_pack, own_seg, own_pos, high_pos, high_cos, high_sin, k, v, na, w_query, w_key, w_value, w_out, d_a, d_h1, gain_a
    )

    def scatter(x, axis, groups, n):
        got = lax.all_to_all(x.reshape((n, x.shape[0] // n) + x.shape[1:]), axis, 0, 0, axis_index_groups=groups, tiled=True)
        return jnp.sum(got.astype(F32), 0).astype(BF)

    def spread(x, axis, groups, n):
        got = lax.all_to_all(jnp.broadcast_to(x[None], (n,) + x.shape), axis, 0, 0, axis_index_groups=groups, tiled=True)
        return got.reshape((n * x.shape[0],) + x.shape[1:])

    def reduce_all(x):
        x = scatter(x, "context", pair_groups, 2)
        x = scatter(x, "expert", None, n_expert)
        x = scatter(x, "context", chip_groups, chips)
        x = spread(x, "context", chip_groups, chips)
        x = spread(x, "expert", None, n_expert)
        return spread(x, "context", pair_groups, 2)

    small = jnp.concatenate([small, g_attn], 0).astype(BF)
    small = jnp.pad(small, ((0, 256 - small.shape[0]), (0, 0)))
    first = reduce_all(g_out).astype(F32)
    last = reduce_all(jnp.concatenate([g_q, g_k, g_v, small], 0)).astype(F32)
    g_q, g_k, g_v, small = last[:width], last[width : 2 * width], last[2 * width : 3 * width], last[3 * width :]
    return (
        result[None], d_tokens[None], small[32], g_q, g_k, g_v, first, small[0],
        small[8 : 8 + experts].T, g_sg, g_su, g_sd, g_eg, g_eu, g_ed,
    )


def solution(mesh):
    rows = P("expert", "context", None)
    owned = P("expert", None, None)
    placed = (rows, P("expert", "context"), rows) + (P(),) * 10 + (owned,) * 3 + (rows,)
    return jax.shard_map(
        per_device, mesh=mesh, in_specs=placed,
        out_specs=(rows, rows) + (P(),) * 10 + (owned,) * 3, check_vma=False,
    )
```
